32 devices in a mesh: tm: 8 (over z, x), space: 4 (over y, core).
Axes of the slice: x: 2, y: 2, z: 4, core: 2. Of those that a mesh axis runs over, the one named last changes fastest.
Arguments:
- features: bfloat16 [16, 24, 32, 256], P('tm', 'space'), may hold values from -6 to 6
- grad_out: bfloat16 [16, 24, 32, 256], P('tm', 'space'), may hold values from -6 to 6
- w_first: bfloat16 [3, 3, 3, 256, 256], replicated, may hold values from -0.078125 to 0.078125
- w_second: bfloat16 [3, 3, 3, 256, 256], replicated, may hold values from -0.078125 to 0.078125
- bias_first: float32 [256], replicated, may hold values from -3 to 3
- clip_start: int32 [8], replicated, may hold values from 0 to 1, as said below
Outputs:
- input_grad: bfloat16 [16, 24, 32, 256], P('tm', 'space')
The draws below stay inside these ranges and needn't reach their ends.
Inputs may be any that keep to these rules, and one draw needn't show every extreme that they name: clip_start is 1 where a time group is the first of its clip and 0 where it continues the clip of the group before it; group 0 begins a clip and group 1 continues it.
All inputs are finite; a program needn't handle non-finite values.
Results may differ from the reference program's by a relative error of at most 0.0024.
Values may be sent and summed in bfloat16 or wider, within the bound.
A program may use at most 64 MiB of HBM per device.

```python
import jax
import jax.numpy as jnp
from jax import lax

C = 256
FR = 2
W = 32
GROUPS = 8
FRAMES = 16
H = 24


def draw_clip_start(key, part):
    picks = jax.random.randint(key, (GROUPS,), 0, 8)
    flags = jnp.where(picks == 0, 1, 0).astype(jnp.int32)
    flags = flags.at[0].set(1)
    flags = flags.at[1].set(0)
    return flags


def block_scale(rng, dims, cuts, smallest, top_value):
    def one(axis_at, blocks):
        steps = jax.random.uniform(jax.random.fold_in(jax.random.fold_in(rng, 6), axis_at), (blocks,), jnp.float32, smallest / len(cuts), top_value / len(cuts))
        return jnp.repeat(jnp.exp(steps), dims[axis_at] // blocks).reshape((-1,) + (1,) * (len(dims) - axis_at - 1))

    loudness = one(*cuts[0])
    for cut in cuts[1:]:
        loudness = loudness * one(*cut)
    return loudness


def noise(own_key, extent, width, limit, shards=(), dtype=jnp.bfloat16):
    array = width * jax.random.normal(own_key, extent, jnp.float32)
    if shards:
        array = array * block_scale(own_key, extent, shards, -0.22, 0.18)
    return jnp.clip(array, -limit, limit).astype(dtype)


def setup_inputs(seed: int = 0) -> dict:
    key_of = jax.random.split(jax.random.key(seed), 7)
    features = noise(key_of[0], (FRAMES, H, W, C), 1.0, 6.0, ((0, 8), (1, 4)))
    grad_out = noise(key_of[1], (FRAMES, H, W, C), 1.0, 6.0, ((0, 8), (1, 4)))
    w_first = noise(key_of[2], (3, 3, 3, C, C), (27 * C) ** -0.5, 0.078125)
    w_second = noise(key_of[3], (3, 3, 3, C, C), (27 * C) ** -0.5, 0.078125)
    bias_first = noise(key_of[4], (C,), 0.7, 3.0, (), jnp.float32)
    clip_start = draw_clip_start(jax.random.fold_in(key_of[6], 71), 0)
    return {"features": features, "grad_out": grad_out, "w_first": w_first, "w_second": w_second, "bias_first": bias_first, "clip_start": clip_start}


def silu_grad(values):
    sigma = jax.nn.sigmoid(values)
    return sigma * (1.0 + values * (1.0 - sigma))

def conv_taps(extended, kernel, frames):
    row_count = extended.shape[1] - 2
    col_count = extended.shape[2] - 2
    channels = extended.shape[3]
    tap_list = [extended[i:i + frames, j:j + row_count, k:k + col_count, :] for i in range(3) for j in range(3) for k in range(3)]
    patches = jnp.concatenate(tap_list, axis=-1)
    product = jnp.dot(patches.reshape(-1, 27 * channels), kernel.reshape(27 * channels, -1), preferred_element_type=jnp.float32)
    return product.reshape(frames, row_count, col_count, -1)

def flipped(kernel):
    return jnp.transpose(kernel[::-1, ::-1, ::-1], (0, 1, 2, 4, 3))

def pad_space(stack):
    return jnp.pad(stack, ((0, 0), (1, 1), (1, 1), (0, 0)))

def reference(features, grad_out, w_first, w_second, bias_first, clip_start):
    group_shape = (GROUPS, FR, H, W, C)
    inputs = features.reshape(group_shape)
    upstream = grad_out.reshape(group_shape)
    carry_on = (1 - clip_start).astype(jnp.bfloat16)
    follows = jnp.concatenate([carry_on[1:], jnp.zeros((1,), jnp.bfloat16)])
    zero_group = jnp.zeros((1, FR, H, W, C), jnp.bfloat16)
    earlier = jnp.concatenate([zero_group, inputs[:-1]]) * carry_on[:, None, None, None, None]
    upcoming = jnp.concatenate([upstream[1:], zero_group]) * follows[:, None, None, None, None]
    flip_first = flipped(w_first)
    flip_second = flipped(w_second)

    def hidden_grad(members):
        previous, current, upstream_part, following = members
        stacked = jnp.concatenate([previous[FR - 2:], current]).astype(jnp.float32)
        active = jax.nn.silu(stacked).astype(jnp.bfloat16)
        hidden = conv_taps(pad_space(active), w_first, FR) + bias_first
        gathered = jnp.concatenate([upstream_part, following[:2]])
        backward = conv_taps(pad_space(gathered), flip_second, FR)
        return (backward * silu_grad(hidden)).astype(jnp.bfloat16)
    g_hidden = lax.map(hidden_grad, (earlier, inputs, upstream, upcoming))
    hidden_next = jnp.concatenate([g_hidden[1:], zero_group]) * follows[:, None, None, None, None]

    def input_grad(members):
        current, upstream_part, current_hidden, following = members
        joined = jnp.concatenate([current_hidden, following[:2]])
        backward = conv_taps(pad_space(joined), flip_first, FR)
        total = upstream_part.astype(jnp.float32) + backward * silu_grad(current.astype(jnp.float32))
        return total.astype(jnp.bfloat16)
    result = lax.map(input_grad, (inputs, upstream, g_hidden, hidden_next))
    return result.reshape(FRAMES, H, W, C)
```

```python
import jax
import jax.numpy as jnp
from jax import lax
from jax.experimental import pallas as pl
from jax.experimental.pallas import tpu as pltpu
from jax.sharding import PartitionSpec as P

MESH = pl.DeviceIdType.MESH
F32 = jnp.float32
BF16 = jnp.bfloat16


def sigmoid(v):
    return 1.0 / (1.0 + jnp.exp(-v))


def silu_grad(v):
    s = sigmoid(v)
    return s * (1.0 + v * (1.0 - s))


def kernel(
    clip_ref, x_ref, g_ref, w1_hbm, w2_hbm, bias_ref, out_ref,
    w1, w2, xv, gv, gh, px, ng, nh, ox, og, oh, rx, rg, rh,
    pa, pg, ph, acc1, acc2, slope, wsem, send_sem, recv_sem,
):
    t, s = lax.axis_index("tm"), lax.axis_index("space")
    tn, sn = lax.axis_size("tm"), lax.axis_size("space")
    frames, rows, cols, ch = xv.shape
    n = rows * cols
    top, bottom = 0, rows - 1
    middle = slice(1, rows - 1)

    def inside(dt, ds):
        ok = None
        for d, at, size in ((dt, t, tn), (ds, s, sn)):
            if d:
                term = (at + d >= 0) if d < 0 else (at + d < size)
                ok = term if ok is None else jnp.logical_and(ok, term)
        return ok

    near = [(dt, ds) for dt in (-1, 0, 1) for ds in (-1, 0, 1) if dt or ds]
    barrier = pltpu.get_barrier_semaphore()
    for dt, ds in near:
        @pl.when(inside(dt, ds))
        def _(dt=dt, ds=ds):
            pl.semaphore_signal(barrier, inc=1, device_id=(t + dt, s + ds), device_id_type=MESH)

    own = [pltpu.make_async_copy(x_ref, xv, wsem.at[6]), pltpu.make_async_copy(g_ref, gv, wsem.at[7])]
    for copy in own:
        copy.start()

    weights = {}
    for i, (hbm, vmem, a) in enumerate(
        [(w1_hbm, w1, 2), (w1_hbm, w1, 1), (w2_hbm, w2, 2), (w2_hbm, w2, 1), (w1_hbm, w1, 0), (w2_hbm, w2, 0)]
    ):
        weights[hbm is w2_hbm, a] = pltpu.make_async_copy(hbm.at[a], vmem.at[a], wsem.at[i])
        weights[hbm is w2_hbm, a].start()

    count = 0
    links = {}

    def link(name, src, dst, dt, ds, via=0):
        nonlocal count
        copy = pltpu.make_async_remote_copy(
            src_ref=src, dst_ref=dst, send_sem=send_sem.at[count], recv_sem=recv_sem.at[count],
            device_id=(t + dt, s + ds), device_id_type=MESH,
        )
        count += 1
        links[name] = (copy, dst, inside(dt or via, ds), inside(-dt or via, -ds))

    for name, src, dst in (("ox", x_ref, ox), ("og", g_ref, og), ("oh", gh, oh)):
        for f in range(2):
            link((name, f, 1), src.at[f, top], dst[f][1], 0, -1)
            link((name, f, 0), src.at[f, bottom], dst[f][0], 0, 1)
    for name, relay, src, dst, through, dt in (
        ("px", "rx", x_ref, px, rx, 1), ("ng", "rg", g_ref, ng, rg, -1), ("nh", "rh", gh, nh, rh, -1)
    ):
        for f in range(2):
            if relay == "rh":
                link((name, f, 2), src.at[f], dst.at[f], dt, 0)
                link((relay, f, 1), src.at[f, top], through[f][1], dt, -1)
                link((relay, f, 0), src.at[f, bottom], through[f][0], dt, 1)
                continue
            link((name, f, 0), src.at[f, top], dst[f][0], dt, 0)
            link((name, f, 1), src.at[f, bottom], dst[f][1], dt, 0)
            link((name, f, 2), src.at[f, middle], dst[f][2], dt, 0)
            link((relay, f, 1), dst[f][0], through[f][1], 0, -1, -dt)
            link((relay, f, 0), dst[f][1], through[f][0], 0, 1, -dt)

    def send(*name):
        copy, dst, going, coming = links[name]
        pl.when(going)(copy.start)

    def arrive(*name):
        copy, dst, going, coming = links[name]
        pl.when(coming)(copy.wait_recv)

        @pl.when(jnp.logical_not(coming))
        def _():
            dst[...] = jnp.zeros(dst.shape, dst.dtype)

    def pass_on(name, relay, f):
        arrive(name, f, 0)
        send(relay, f, 1)
        arrive(name, f, 1)
        send(relay, f, 0)

    total = 1
    for lo, hi in ((inside(-1, 0), inside(1, 0)), (inside(0, -1), inside(0, 1))):
        total = total * (1 + lo.astype(jnp.int32) + hi.astype(jnp.int32))
    pl.semaphore_wait(barrier, total - 1)
    for name in ("px", "ng"):
        for f in range(2):
            for part in range(2):
                send(name, f, part)
    for f in (1, 0):
        send("px", f, 2)
    for f in (0, 1):
        send("ng", f, 2)
    for name in ("ox", "og"):
        for f in range(2):
            send(name, f, 0)
            send(name, f, 1)
    keep_prev = (1 - clip_ref[t]).astype(F32)
    keep_next = (1 - clip_ref[jnp.minimum(t + 1, tn - 1)]).astype(F32)

    def spread(dst, frame, row, val, forward):
        col = lax.broadcasted_iota(jnp.int32, val.shape, 0) % cols
        size = val.shape[0]
        left = jnp.where(col == 0, 0.0, pltpu.roll(val, 1, 0))
        right = jnp.where(col == cols - 1, 0.0, pltpu.roll(val, size - 1, 0))
        parts = (left, val, right) if forward else (right, val, left)
        height = size // cols
        for k, part in enumerate(parts):
            dst[frame, row:row + height, :, k * ch:(k + 1) * ch] = part.astype(BF16).reshape(height, cols, ch)

    def load(ref):
        return ref[...].astype(F32).reshape(-1, ch)

    def fill(dst, frame, row, ref, forward, keep=None):
        v = load(ref)
        if forward:
            v = (v * sigmoid(v)).astype(BF16).astype(F32)
        spread(dst, frame, row, v if keep is None else v * keep, forward)

    def taps(buf, w, frame, k, a, forward):
        sum_ = None
        for b in range(3):
            r = b if forward else 2 - b
            lhs = buf[frame:frame + k, r:r + rows].reshape(k * n, 3 * ch)
            if forward:
                rhs = w[a, b].reshape(3 * ch, ch)
                term = jnp.dot(lhs, rhs, preferred_element_type=F32)
            else:
                rhs = jnp.concatenate([w[a, b, c] for c in range(3)], axis=1)
                term = lax.dot_general(lhs, rhs, (((1,), (1,)), ((), ())), preferred_element_type=F32)
            sum_ = term if sum_ is None else sum_ + term
        return sum_

    def own_fill(dst, frame, f, name, ref, halo, forward):
        fill(dst, frame, 1, ref.at[f], forward)
        for side, row in ((0, 0), (1, rows + 1)):
            arrive(name, f, side)
            fill(dst, frame, row, halo[f][side], forward)

    def far_fill(dst, frame, f, name, relay, parts, halo, forward, keep):
        if relay == "rh":
            arrive(name, f, 2)
            fill(dst, frame, 1, parts.at[f], forward, keep)
        for part, row in () if relay == "rh" else ((0, 1), (1, rows), (2, 2)):
            if part == 2:
                arrive(name, f, 2)
            fill(dst, frame, row, parts[f][part], forward, keep)
        for side, row in ((0, 0), (1, rows + 1)):
            arrive(relay, f, side)
            fill(dst, frame, row, halo[f][side], forward, keep)

    for copy in own:
        copy.wait()
    for f in range(2):
        own_fill(pa, 2 + f, f, "ox", xv, ox, True)
    weights[False, 2].wait()
    acc1[...] = taps(pa, w1, 2, 2, 2, True) + bias_ref[...]
    pass_on("px", "rx", 1)
    weights[False, 1].wait()
    acc1[n:] += taps(pa, w1, 2, 1, 1, True)
    pass_on("px", "rx", 0)
    for f in range(2):
        own_fill(pg, f, f, "og", gv, og, False)
    weights[True, 2].wait()
    acc2[...] = taps(pg, w2, 0, 2, 2, False)
    pass_on("ng", "rg", 0)
    weights[True, 1].wait()
    acc2[:n] += taps(pg, w2, 1, 1, 1, False)

    far_fill(pa, 1, 1, "px", "rx", px, rx, True, keep_prev)
    acc1[:n] += taps(pa, w1, 1, 1, 1, True)
    for f in range(2):
        slope[f * n:(f + 1) * n] = silu_grad(load(xv.at[f]))
    far_fill(pa, 0, 0, "px", "rx", px, rx, True, keep_prev)
    weights[False, 0].wait()
    acc1[...] = silu_grad(acc1[...] + taps(pa, w1, 0, 2, 0, True))

    def hidden_out(f, backward):
        val = backward * acc1[f * n:(f + 1) * n]
        gh[f] = val.astype(BF16).reshape(rows, cols, ch)
        for side in range(2):
            send("rh", f, side)
        for side in range(2):
            send("oh", f, side)
        send("nh", f, 2)

    far_fill(pg, 2, 0, "ng", "rg", ng, rg, False, keep_next)
    weights[True, 0].wait()
    hidden_out(0, acc2[:n] + taps(pg, w2, 2, 1, 0, False))
    pass_on("ng", "rg", 1)
    acc2[n:] += taps(pg, w2, 2, 1, 1, False)
    far_fill(pg, 3, 1, "ng", "rg", ng, rg, False, keep_next)
    hidden_out(1, acc2[n:] + taps(pg, w2, 3, 1, 0, False))

    own_fill(ph, 0, 0, "oh", gh, oh, False)
    own_fill(ph, 1, 1, "oh", gh, oh, False)
    acc1[...] = taps(ph, w1, 0, 2, 2, False)
    acc1[:n] += taps(ph, w1, 1, 1, 1, False)

    def result(f, backward):
        val = load(gv.at[f]) + backward * slope[f * n:(f + 1) * n]
        out_ref[f] = val.astype(BF16).reshape(rows, cols, ch)

    far_fill(ph, 2, 0, "nh", "rh", nh, rh, False, keep_next)
    result(0, acc1[:n] + taps(ph, w1, 2, 1, 0, False))
    acc1[n:] += taps(ph, w1, 2, 1, 1, False)
    far_fill(ph, 3, 1, "nh", "rh", nh, rh, False, keep_next)
    result(1, acc1[n:] + taps(ph, w1, 3, 1, 0, False))
    for copy, dst, going, coming in links.values():
        pl.when(going)(copy.wait_send)


def local(features, grad_out, w_first, w_second, bias_first, clip_start):
    frames, rows, cols, ch = features.shape
    group = pltpu.VMEM((frames, rows, cols, ch), BF16)
    line = pltpu.VMEM((cols, ch), BF16)
    inner = pltpu.VMEM((rows - 2, cols, ch), BF16)
    pairs = [[line, line], [line, line]]
    thirds = [[line, line, inner], [line, line, inner]]
    wide = pltpu.VMEM((2 * frames, rows + 2, cols, 3 * ch), BF16)
    wsize = pltpu.VMEM(w_first.shape, BF16)
    acc = pltpu.VMEM((frames * rows * cols, ch), F32)
    vmem = pl.BlockSpec(memory_space=pltpu.VMEM)
    hbm = pl.BlockSpec(memory_space=pl.ANY)
    return pl.pallas_call(
        kernel,
        out_shape=pltpu.VMEM(features.shape, features.dtype),
        in_specs=[pl.BlockSpec(memory_space=pltpu.SMEM), hbm, hbm, hbm, hbm, vmem],
        out_specs=vmem,
        scratch_shapes=[
            wsize, wsize, group, group, group,
            thirds, thirds, group, pairs, pairs, pairs, pairs, pairs, pairs,
            wide, wide, wide, acc, acc, acc,
            pltpu.SemaphoreType.DMA((8,)),
            pltpu.SemaphoreType.DMA((42,)),
            pltpu.SemaphoreType.DMA((42,)),
        ],
        compiler_params=pltpu.CompilerParams(
            collective_id=0, has_side_effects=True, vmem_limit_bytes=54 * 1024 * 1024
        ),
    )(clip_start, features, grad_out, w_first, w_second, bias_first.reshape(1, ch))


def solution(mesh):
    placed = (P("tm", "space", None, None), P("tm", "space", None, None), P(), P(), P(), P())
    return jax.shard_map(
        local, mesh=mesh, in_specs=placed, out_specs=P("tm", "space", None, None), check_vma=False
    )
```

```python
import jax
import jax.numpy as jnp
from jax import lax
from jax.experimental import pallas as pl
from jax.experimental.pallas import tpu as pltpu
from jax.sharding import PartitionSpec as P

MESH = pl.DeviceIdType.MESH
F32 = jnp.float32
BF16 = jnp.bfloat16

FORWARD_OWN = ((2, 0, 2, 2), (1, 1, 2, 1))
FORWARD_FAR = ((0, 0, 0, 2), (1, 0, 1, 1))
BACKWARD_OWN = ((2, 0, 0, 2), (1, 0, 1, 1))
BACKWARD_FAR = ((0, 0, 2, 2), (1, 1, 2, 1))


def sigmoid(v):
    return 1.0 / (1.0 + jnp.exp(-v))


def silu_grad(v):
    s = sigmoid(v)
    return s * (1.0 + v * (1.0 - s))


def kernel(
    clip_ref, x_ref, g_ref, w1_hbm, w2_hbm, bias_ref, out_ref,
    w1, w2, t1, t2, xw, aw, gw, hw, acc1, acc2, acc3, slope, local_sem, send_sem, recv_sem,
):
    t, s = lax.axis_index("tm"), lax.axis_index("space")
    tn, sn = lax.axis_size("tm"), lax.axis_size("space")
    frames, rows, cols, ch = x_ref.shape
    last = rows - 1

    def inside(dt, ds):
        ok = None
        for d, at, size in ((dt, t, tn), (ds, s, sn)):
            if d:
                term = (at + d >= 0) if d < 0 else (at + d < size)
                ok = term if ok is None else jnp.logical_and(ok, term)
        return ok

    barrier = pltpu.get_barrier_semaphore()
    peers = 0
    for dt, ds in ((1, 0), (-1, 0), (0, 1), (0, -1)):
        @pl.when(inside(dt, ds))
        def _(dt=dt, ds=ds):
            pl.semaphore_signal(barrier, inc=1, device_id=(t + dt, s + ds), device_id_type=MESH)
        peers = peers + inside(dt, ds).astype(jnp.int32)

    x_own, g_own, h_own = xw.at[2:4], gw.at[0:2], hw.at[0:2]
    x_far, g_far, h_far = xw.at[0:2], gw.at[2:4], hw.at[2:4]
    inner = pl.ds(1, rows)
    own = [
        pltpu.make_async_copy(x_ref, x_own.at[:, inner], local_sem.at[0]),
        pltpu.make_async_copy(g_ref, g_own.at[:, inner], local_sem.at[1]),
    ]
    for copy in own:
        copy.start()
    weights = {}
    for i, (hbm, vmem, a) in enumerate(
        ((w2_hbm, w2, 2), (w2_hbm, w2, 1), (w1_hbm, w1, 2), (w1_hbm, w1, 1), (w2_hbm, w2, 0), (w1_hbm, w1, 0))
    ):
        weights[hbm is w2_hbm, a] = pltpu.make_async_copy(hbm.at[a], vmem.at[a], local_sem.at[2 + i])
        weights[hbm is w2_hbm, a].start()

    links = {}

    def link(name, src, dst, dt, ds, via=0):
        count = len(links)
        copy = pltpu.make_async_remote_copy(
            src_ref=src, dst_ref=dst, send_sem=send_sem.at[count], recv_sem=recv_sem.at[count],
            device_id=(t + dt, s + ds), device_id_type=MESH,
        )
        links[name] = (copy, dst, inside(dt or via, ds), inside(-dt or via, -ds))

    spans = {"top": (1, 1), "bottom": (rows, 1), "upper": (2, 1), "lower": (rows - 1, 1), "middle": (3, rows - 4), "inner": (2, rows - 2)}
    for name, src, off, near_w, far_w, dt in (
        ("x", x_ref, 1, x_own, x_far, 1), ("g", g_ref, 1, g_own, g_far, -1), ("h", h_own, 0, h_own, h_far, -1)
    ):
        for part in ("top", "bottom") + (("inner",) if name == "h" else ("upper", "lower", "middle")):
            at, size = spans[part]
            link((name, part), src.at[:, pl.ds(at - off, size)], far_w.at[:, pl.ds(at, size)], dt, 0)
        for part, ds, to in (("top", -1, rows + 1), ("bottom", 1, 0)):
            at, size = spans[part]
            link((name, "own", to), src.at[:, pl.ds(at - off, 1)], near_w.at[:, pl.ds(to, 1)], 0, ds)
            link((name, "far", to), far_w.at[:, pl.ds(at, 1)], far_w.at[:, pl.ds(to, 1)], 0, ds, -dt)

    def send(*name):
        copy, dst, going, coming = links[name]
        pl.when(going)(copy.start)

    def arrive(*name):
        copy, dst, going, coming = links[name]
        pl.when(coming)(copy.wait_recv)

        @pl.when(jnp.logical_not(coming))
        def _():
            dst[...] = jnp.zeros(dst.shape, dst.dtype)

    def halos(name, which):
        for to in (0, rows + 1):
            arrive(name, which, to)

    def pass_on(name):
        for part, to in (("top", rows + 1), ("bottom", 0)):
            arrive(name, part)
            send(name, "far", to)

    keep_prev = (1 - clip_ref[t]).astype(F32)
    keep_next = (1 - clip_ref[jnp.minimum(t + 1, tn - 1)]).astype(F32)

    def activate(e, at, size, keep=None):
        v = xw[e:e + 2, at:at + size].astype(F32)
        v = v * sigmoid(v)
        aw[e:e + 2, at:at + size] = (v if keep is None else v * keep).astype(BF16)

    def products(buf, w, a, b, e, k, chunks):
        parts = [buf[e:e + k, at:at + n].reshape(k * n * cols, ch) for at, n in chunks]
        lhs = parts[0] if len(parts) == 1 else jnp.concatenate(parts, axis=0)
        return [jnp.dot(lhs, w[a, b, c], preferred_element_type=F32) for c in range(3)]

    def turn(b, forward):
        return b if forward else 2 - b

    def store(acc, buf, w, taps, forward, first, at, n, keep=None):
        for a, f, e, k in taps:
            sums = None
            for b in range(3):
                new = products(buf, w, a, turn(b, forward), e, k, [(o + b, m) for o, m in zip(at, n)])
                sums = new if sums is None else [x + y for x, y in zip(sums, new)]
            put(acc, sums, f, k, list(zip(at, n)), first and k == 2, keep)

    def put(acc, sums, f, k, outs, first, keep):
        for c in range(3):
            begin = 0
            for o, n in outs:
                size = k * n * cols
                val = sums[c][begin:begin + size]
                begin += size
                if keep is not None:
                    val = val * keep
                val = val.reshape(k, n, cols, ch)
                ref = acc.at[f:f + k, o:o + n, :, c * ch:(c + 1) * ch]
                ref[...] = val if first else ref[...] + val

    def scatter(acc, buf, w, taps, forward, maps, keep):
        for a, f, e, k in taps:
            for b in range(3):
                sums = products(buf, w, a, turn(b, forward), e, k, maps[b])
                put(acc, sums, f, k, [(at - b, n) for at, n in maps[b]], False, keep)

    def total(acc, forward, at, n):
        m = frames * n * cols
        parts = [acc[:, at:at + n, :, c * ch:(c + 1) * ch].reshape(m, ch) for c in range(3)]
        left, right = (parts[0], parts[2]) if forward else (parts[2], parts[0])
        col = lax.broadcasted_iota(jnp.int32, (m, ch), 0) % cols
        left = jnp.where(col == 0, 0.0, pltpu.roll(left, 1, 0))
        right = jnp.where(col == cols - 1, 0.0, pltpu.roll(right, m - 1, 0))
        return parts[1] + left + right

    def flip(w, wt, a):
        for b in range(3):
            for c in range(3):
                wt[a, b, c] = w[a, b, c].T

    pl.semaphore_wait(barrier, peers)
    for part in ("top", "bottom"):
        send("x", part)
        send("g", part)
    for part in ("upper", "lower", "middle"):
        send("x", part)
        send("g", part)
        if part == "upper":
            for name in ("x", "g"):
                for to in (0, rows + 1):
                    send(name, "own", to)
    for copy in own:
        copy.wait()
    activate(2, 1, rows)
    weights[True, 2].wait()
    flip(w2, t2, 2)
    weights[True, 1].wait()
    flip(w2, t2, 1)
    halos("x", "own")
    activate(2, 0, 1)
    activate(2, rows + 1, 1)
    weights[False, 2].wait()
    weights[False, 1].wait()
    store(acc1, aw, w1, FORWARD_OWN, True, True, [0], [rows])
    pass_on("x")
    pass_on("g")
    halos("g", "own")
    store(acc2, gw, t2, BACKWARD_OWN, False, True, [0], [rows])
    weights[True, 0].wait()
    flip(w2, t2, 0)
    weights[False, 0].wait()
    for a in (2, 1, 0):
        flip(w1, t1, a)
    slope[...] = silu_grad(xw[2:4, 1:rows + 1].astype(F32))
    activate(0, 1, 1, keep_prev)
    activate(0, rows, 1, keep_prev)
    halos("x", "far")
    activate(0, 0, 1, keep_prev)
    activate(0, rows + 1, 1, keep_prev)
    for part, at in (("upper", 2), ("lower", rows - 1)):
        arrive("x", part)
        activate(0, at, 1, keep_prev)

    edge_rows = ([0, last], [1, 1])
    store(acc1, aw, w1, FORWARD_FAR, True, False, *edge_rows)
    halos("g", "far")
    arrive("g", "upper")
    arrive("g", "lower")
    store(acc2, gw, t2, BACKWARD_FAR, False, False, *edge_rows, keep_next)

    def hidden(at, n):
        hid = total(acc1, True, at, n) + bias_ref[...]
        val = total(acc2, False, at, n) * silu_grad(hid)
        hw[0:2, at + 1:at + 1 + n] = val.astype(BF16).reshape(frames, n, cols, ch)

    hidden(0, 1)
    send("h", "top")
    send("h", "own", rows + 1)
    hidden(last, 1)
    send("h", "bottom")
    send("h", "own", 0)

    early = ([(1, 2)], [(2, 1), (rows - 1, 1)], [(rows - 1, 2)])
    scatter(acc1, aw, w1, FORWARD_FAR, True, early, None)
    scatter(acc2, gw, t2, BACKWARD_FAR, False, early, keep_next)
    late = ([(3, rows - 4)],) * 3
    arrive("x", "middle")
    activate(0, 3, rows - 4, keep_prev)
    scatter(acc1, aw, w1, FORWARD_FAR, True, late, None)
    arrive("g", "middle")
    scatter(acc2, gw, t2, BACKWARD_FAR, False, late, keep_next)
    hidden(1, rows - 2)
    send("h", "inner")

    halos("h", "own")
    store(acc3, hw, t1, BACKWARD_OWN, False, True, [0], [rows])
    pass_on("h")
    halos("h", "far")
    scatter(acc3, hw, t1, BACKWARD_FAR, False, ([(0, 2)], [(1, 1), (rows, 1)], [(rows, 2)]), keep_next)
    arrive("h", "inner")
    scatter(acc3, hw, t1, BACKWARD_FAR, False, ([(2, rows - 2)],) * 3, keep_next)
    back = total(acc3, False, 0, rows).reshape(frames, rows, cols, ch)
    out_ref[...] = (gw[0:2, 1:rows + 1].astype(F32) + back * slope[...]).astype(BF16)
    for copy, dst, going, coming in links.values():
        pl.when(going)(copy.wait_send)


def local(features, grad_out, w_first, w_second, bias_first, clip_start):
    frames, rows, cols, ch = features.shape
    window = pltpu.VMEM((2 * frames, rows + 2, cols, ch), BF16)
    wsize = pltpu.VMEM(w_first.shape, BF16)
    acc = pltpu.VMEM((frames, rows, cols, 3 * ch), F32)
    vmem = pl.BlockSpec(memory_space=pltpu.VMEM)
    hbm = pl.BlockSpec(memory_space=pl.ANY)
    return pl.pallas_call(
        kernel,
        out_shape=pltpu.VMEM(features.shape, features.dtype),
        in_specs=[pl.BlockSpec(memory_space=pltpu.SMEM), hbm, hbm, hbm, hbm, vmem],
        out_specs=vmem,
        scratch_shapes=[
            wsize, wsize, wsize, wsize, window, window, window, window,
            acc, acc, acc, pltpu.VMEM((frames, rows, cols, ch), F32),
            pltpu.SemaphoreType.DMA((8,)),
            pltpu.SemaphoreType.DMA((25,)),
            pltpu.SemaphoreType.DMA((25,)),
        ],
        compiler_params=pltpu.CompilerParams(
            collective_id=0, has_side_effects=True, vmem_limit_bytes=54 * 1024 * 1024
        ),
    )(clip_start, features, grad_out, w_first, w_second, bias_first.reshape(1, ch))


def solution(mesh):
    placed = (P("tm", "space", None, None), P("tm", "space", None, None), P(), P(), P(), P())
    return jax.shard_map(
        local, mesh=mesh, in_specs=placed, out_specs=P("tm", "space", None, None), check_vma=False
    )
```

```python
import jax
import jax.numpy as jnp
from jax import lax
from jax.experimental import pallas as pl
from jax.experimental.pallas import tpu as pltpu
from jax.sharding import PartitionSpec as P

MESH = pl.DeviceIdType.MESH
F32 = jnp.float32
BF16 = jnp.bfloat16

FORWARD_OWN = ((2, 0, 2, 2), (1, 1, 2, 1))
FORWARD_FAR = ((0, 0, 0, 2), (1, 0, 1, 1))
BACKWARD_OWN = ((2, 0, 0, 2), (1, 0, 1, 1))
BACKWARD_FAR = ((0, 0, 2, 2), (1, 1, 2, 1))


def sigmoid(v):
    return 1.0 / (1.0 + jnp.exp(-v))


def silu_grad(v):
    s = sigmoid(v)
    return s * (1.0 + v * (1.0 - s))


def kernel(
    clip_ref, x_ref, g_ref, w1_hbm, w2_hbm, bias_ref, out_ref,
    w1, w2, t1, t2, xw, aw, gw, hw, acc1, acc2, acc3, slope, local_sem, send_sem, recv_sem,
):
    t, s = lax.axis_index("tm"), lax.axis_index("space")
    tn, sn = lax.axis_size("tm"), lax.axis_size("space")
    frames, rows, cols, ch = x_ref.shape
    last = rows - 1

    def inside(dt, ds):
        ok = None
        for d, at, size in ((dt, t, tn), (ds, s, sn)):
            if d:
                term = (at + d >= 0) if d < 0 else (at + d < size)
                ok = term if ok is None else jnp.logical_and(ok, term)
        return ok

    barrier = pltpu.get_barrier_semaphore()
    peers = 0
    for dt, ds in ((1, 0), (-1, 0), (0, 1), (0, -1)):
        @pl.when(inside(dt, ds))
        def _(dt=dt, ds=ds):
            pl.semaphore_signal(barrier, inc=1, device_id=(t + dt, s + ds), device_id_type=MESH)
        peers = peers + inside(dt, ds).astype(jnp.int32)

    x_own, g_own, h_own = xw.at[2:4], gw.at[0:2], hw.at[0:2]
    x_far, g_far, h_far = xw.at[0:2], gw.at[2:4], hw.at[2:4]
    inner = pl.ds(1, rows)
    own = [
        pltpu.make_async_copy(x_ref, x_own.at[:, inner], local_sem.at[0]),
        pltpu.make_async_copy(g_ref, g_own.at[:, inner], local_sem.at[1]),
    ]
    for copy in own:
        copy.start()
    weights = {}
    for i, (hbm, vmem, a) in enumerate(
        ((w1_hbm, w1, 2), (w1_hbm, w1, 1), (w2_hbm, w2, 1), (w2_hbm, w2, 2), (w2_hbm, w2, 0), (w1_hbm, w1, 0))
    ):
        weights[hbm is w2_hbm, a] = pltpu.make_async_copy(hbm.at[a], vmem.at[a], local_sem.at[2 + i])
        weights[hbm is w2_hbm, a].start()

    links = {}

    def link(name, src, dst, dt, ds, via=0):
        count = len(links)
        copy = pltpu.make_async_remote_copy(
            src_ref=src, dst_ref=dst, send_sem=send_sem.at[count], recv_sem=recv_sem.at[count],
            device_id=(t + dt, s + ds), device_id_type=MESH,
        )
        links[name] = (copy, dst, inside(dt or via, ds), inside(-dt or via, -ds))

    spans = {"top": (1, 1), "bottom": (rows, 1), "upper": (2, 1), "lower": (rows - 1, 1), "middle": (3, rows - 4)}
    for name, src, off, near_w, far_w, dt in (
        ("x", x_ref, 1, x_own, x_far, 1), ("g", g_ref, 1, g_own, g_far, -1), ("h", h_own, 0, h_own, h_far, -1)
    ):
        for part in ("top", "bottom", "upper", "lower", "middle"):
            at, size = spans[part]
            link((name, part), src.at[:, pl.ds(at - off, size)], far_w.at[:, pl.ds(at, size)], dt, 0)
        for part, ds, to in (("top", -1, rows + 1), ("bottom", 1, 0)):
            at, size = spans[part]
            link((name, "own", to), src.at[:, pl.ds(at - off, 1)], near_w.at[:, pl.ds(to, 1)], 0, ds)
            link((name, "far", to), far_w.at[:, pl.ds(at, 1)], far_w.at[:, pl.ds(to, 1)], 0, ds, -dt)

    def send(*name):
        copy, dst, going, coming = links[name]
        pl.when(going)(copy.start)

    def arrive(*name):
        copy, dst, going, coming = links[name]
        pl.when(coming)(copy.wait_recv)

        @pl.when(jnp.logical_not(coming))
        def _():
            dst[...] = jnp.zeros(dst.shape, dst.dtype)

    def halos(name, which):
        for to in (0, rows + 1):
            arrive(name, which, to)

    def pass_on(name):
        for part, to in (("top", rows + 1), ("bottom", 0)):
            arrive(name, part)
            send(name, "far", to)

    keep_prev = (1 - clip_ref[t]).astype(F32)
    keep_next = (1 - clip_ref[jnp.minimum(t + 1, tn - 1)]).astype(F32)

    def activate(e, at, size, keep=None):
        v = xw[e:e + 2, at:at + size].astype(F32)
        v = v * sigmoid(v)
        aw[e:e + 2, at:at + size] = (v if keep is None else v * keep).astype(BF16)

    def products(buf, w, a, b, e, k, chunks):
        w, wt = w
        parts = [buf[e:e + k, at:at + n].reshape(k * n * cols, ch) for at, n in chunks]
        lhs = parts[0] if len(parts) == 1 else jnp.concatenate(parts, axis=0)
        if wt is not None and a == 2:
            dims = (((1,), (1,)), ((), ()))
            return [lax.dot_general(lhs, w[a, b, c], dims, preferred_element_type=F32) for c in range(3)]
        return [jnp.dot(lhs, (w if wt is None else wt)[a, b, c], preferred_element_type=F32) for c in range(3)]

    first, second, third = (w1, None), (w2, t2), (w1, t1)

    def turn(b, forward):
        return b if forward else 2 - b

    def store(acc, buf, w, taps, forward, fresh, at, n, keep=None):
        for a, f, e, k in taps:
            sums = None
            for b in range(3):
                new = products(buf, w, a, turn(b, forward), e, k, [(o + b, m) for o, m in zip(at, n)])
                sums = new if sums is None else [x + y for x, y in zip(sums, new)]
            put(acc, sums, f, k, list(zip(at, n)), fresh and k == 2, keep)

    def put(acc, sums, f, k, outs, fresh, keep):
        for c in range(3):
            begin = 0
            for o, n in outs:
                size = k * n * cols
                val = sums[c][begin:begin + size]
                begin += size
                if keep is not None:
                    val = val * keep
                val = val.reshape(k, n, cols, ch)
                ref = acc.at[f:f + k, o:o + n, :, c * ch:(c + 1) * ch]
                ref[...] = val if fresh else ref[...] + val

    def spread(acc, buf, w, taps, forward, sources, outs, keep=None):
        for a, f, e, k in taps:
            terms = {}
            for b in range(3):
                here = [r for r in sources if r - b in outs]
                if not here:
                    continue
                vals = products(buf, w, a, turn(b, forward), e, k, [(r, 1) for r in here])
                for at, r in enumerate(here):
                    piece = slice(at * k * cols, (at + 1) * k * cols)
                    for c in range(3):
                        terms.setdefault((c, r - b), []).append(vals[c][piece])
            for (c, o), vals in sorted(terms.items()):
                val = sum(vals[1:], vals[0])
                if keep is not None:
                    val = val * keep
                ref = acc.at[f:f + k, o, :, c * ch:(c + 1) * ch]
                ref[...] = ref[...] + val.reshape(k, cols, ch)

    def total(acc, forward, at, n):
        m = frames * n * cols
        parts = [acc[:, at:at + n, :, c * ch:(c + 1) * ch].reshape(m, ch) for c in range(3)]
        left, right = (parts[0], parts[2]) if forward else (parts[2], parts[0])
        col = lax.broadcasted_iota(jnp.int32, (m, ch), 0) % cols
        left = jnp.where(col == 0, 0.0, pltpu.roll(left, 1, 0))
        right = jnp.where(col == cols - 1, 0.0, pltpu.roll(right, m - 1, 0))
        return parts[1] + left + right

    def flip(w, wt, a):
        for b in range(3):
            for c in range(3):
                wt[a, b, c] = w[a, b, c].T

    pl.semaphore_wait(barrier, peers)
    for part in ("top", "bottom"):
        send("x", part)
        send("g", part)
    for part in ("upper", "lower", "middle"):
        send("x", part)
        send("g", part)
        if part == "upper":
            for name in ("x", "g"):
                for to in (0, rows + 1):
                    send(name, "own", to)
    for copy in own:
        copy.wait()
    activate(2, 1, rows)
    halos("x", "own")
    activate(2, 0, 1)
    activate(2, rows + 1, 1)
    weights[False, 2].wait()
    weights[False, 1].wait()
    store(acc1, aw, first, FORWARD_OWN, True, True, [0], [rows])
    weights[True, 1].wait()
    flip(w2, t2, 1)
    halos("g", "own")
    weights[True, 2].wait()
    store(acc2, gw, second, BACKWARD_OWN, False, True, [0], [rows])
    pass_on("x")
    pass_on("g")
    weights[True, 0].wait()
    flip(w2, t2, 0)
    weights[False, 0].wait()
    slope[...] = silu_grad(xw[2:4, 1:rows + 1].astype(F32))
    activate(0, 1, 1, keep_prev)
    activate(0, rows, 1, keep_prev)

    every = range(rows)
    edges, inside_rows = (0, last), range(1, last)
    near_rows, mid_rows = (1, 2, rows - 1, rows), range(3, rows - 1)
    outer = (0,) + near_rows + (rows + 1,)
    halos("x", "far")
    activate(0, 0, 1, keep_prev)
    activate(0, rows + 1, 1, keep_prev)
    for part, at in (("upper", 2), ("lower", rows - 1)):
        arrive("x", part)
        activate(0, at, 1, keep_prev)
    spread(acc1, aw, first, FORWARD_FAR, True, outer, edges)
    halos("g", "far")
    arrive("g", "upper")
    arrive("g", "lower")
    spread(acc2, gw, second, BACKWARD_FAR, False, outer, edges, keep_next)

    def hidden(at, n):
        hid = total(acc1, True, at, n) + bias_ref[...]
        val = total(acc2, False, at, n) * silu_grad(hid)
        hw[0:2, at + 1:at + 1 + n] = val.astype(BF16).reshape(frames, n, cols, ch)

    hidden(0, 1)
    hidden(last, 1)
    send("h", "top")
    send("h", "bottom")
    send("h", "own", rows + 1)
    send("h", "own", 0)
    spread(acc1, aw, first, FORWARD_FAR, True, near_rows, inside_rows)
    spread(acc2, gw, second, BACKWARD_FAR, False, near_rows, inside_rows, keep_next)

    arrive("x", "middle")
    activate(0, 3, rows - 4, keep_prev)
    spread(acc1, aw, first, FORWARD_FAR, True, mid_rows, every)
    arrive("g", "middle")
    spread(acc2, gw, second, BACKWARD_FAR, False, mid_rows, every, keep_next)
    hidden(1, rows - 2)
    send("h", "upper")
    send("h", "lower")
    send("h", "middle")

    flip(w1, t1, 1)
    halos("h", "own")
    store(acc3, hw, third, BACKWARD_OWN, False, True, [0], [rows])
    pass_on("h")
    flip(w1, t1, 0)
    arrive("h", "upper")
    arrive("h", "lower")
    halos("h", "far")
    spread(acc3, hw, third, BACKWARD_FAR, False, outer, every, keep_next)

    def result(at, n):
        back = total(acc3, False, at, n).reshape(frames, n, cols, ch)
        own_g = gw[0:2, at + 1:at + 1 + n].astype(F32)
        out_ref[:, at:at + n] = (own_g + back * slope[:, at:at + n]).astype(BF16)

    result(0, 1)
    result(last, 1)
    arrive("h", "middle")
    spread(acc3, hw, third, BACKWARD_FAR, False, mid_rows, every, keep_next)
    result(1, rows - 2)
    for copy, dst, going, coming in links.values():
        pl.when(going)(copy.wait_send)


def local(features, grad_out, w_first, w_second, bias_first, clip_start):
    frames, rows, cols, ch = features.shape
    window = pltpu.VMEM((2 * frames, rows + 2, cols, ch), BF16)
    wsize = pltpu.VMEM(w_first.shape, BF16)
    acc = pltpu.VMEM((frames, rows, cols, 3 * ch), F32)
    vmem = pl.BlockSpec(memory_space=pltpu.VMEM)
    hbm = pl.BlockSpec(memory_space=pl.ANY)
    return pl.pallas_call(
        kernel,
        out_shape=pltpu.VMEM(features.shape, features.dtype),
        in_specs=[pl.BlockSpec(memory_space=pltpu.SMEM), hbm, hbm, hbm, hbm, vmem],
        out_specs=vmem,
        scratch_shapes=[
            wsize, wsize, wsize, wsize, window, window, window, window,
            acc, acc, acc, pltpu.VMEM((frames, rows, cols, ch), F32),
            pltpu.SemaphoreType.DMA((8,)),
            pltpu.SemaphoreType.DMA((27,)),
            pltpu.SemaphoreType.DMA((27,)),
        ],
        compiler_params=pltpu.CompilerParams(
            collective_id=0, has_side_effects=True, vmem_limit_bytes=54 * 1024 * 1024
        ),
    )(clip_start, features, grad_out, w_first, w_second, bias_first.reshape(1, ch))


def solution(mesh):
    placed = (P("tm", "space", None, None), P("tm", "space", None, None), P(), P(), P(), P())
    return jax.shard_map(
        local, mesh=mesh, in_specs=placed, out_specs=P("tm", "space", None, None), check_vma=False
    )
```

```python
import jax
import jax.numpy as jnp
from jax import lax
from jax.experimental import pallas as pl
from jax.experimental.pallas import tpu as pltpu
from jax.sharding import PartitionSpec as P

MESH = pl.DeviceIdType.MESH
F32 = jnp.float32
BF16 = jnp.bfloat16

FORWARD_OWN = ((2, 0, 2, 2), (1, 1, 2, 1))
FORWARD_FAR = ((0, 0, 0, 2), (1, 0, 1, 1))
BACKWARD_OWN = ((2, 0, 0, 2), (1, 0, 1, 1))
BACKWARD_FAR = ((0, 0, 2, 2), (1, 1, 2, 1))


def sigmoid(v):
    return 1.0 / (1.0 + jnp.exp(-v))


def silu_grad(v):
    s = sigmoid(v)
    return s * (1.0 + v * (1.0 - s))


def kernel(
    clip_ref, x_ref, g_ref, w1_hbm, w2_hbm, bias_ref, out_ref,
    w1, w2, t1, t2, xw, aw, gw, hw, acc1, acc2, acc3, slope, local_sem, send_sem, recv_sem,
):
    t, s = lax.axis_index("tm"), lax.axis_index("space")
    tn, sn = lax.axis_size("tm"), lax.axis_size("space")
    frames, rows, cols, ch = x_ref.shape
    last = rows - 1

    def inside(dt, ds):
        ok = None
        for d, at, size in ((dt, t, tn), (ds, s, sn)):
            if d:
                term = (at + d >= 0) if d < 0 else (at + d < size)
                ok = term if ok is None else jnp.logical_and(ok, term)
        return ok

    barrier = pltpu.get_barrier_semaphore()
    peers = 0
    for dt, ds in ((1, 0), (-1, 0), (0, 1), (0, -1)):
        @pl.when(inside(dt, ds))
        def _(dt=dt, ds=ds):
            pl.semaphore_signal(barrier, inc=1, device_id=(t + dt, s + ds), device_id_type=MESH)
        peers = peers + inside(dt, ds).astype(jnp.int32)

    x_own, g_own, h_own = xw.at[2:4], gw.at[0:2], hw.at[0:2]
    x_far, g_far, h_far = xw.at[0:2], gw.at[2:4], hw.at[2:4]
    inner = pl.ds(1, rows)
    own = [
        pltpu.make_async_copy(x_ref, x_own.at[:, inner], local_sem.at[0]),
        pltpu.make_async_copy(g_ref, g_own.at[:, inner], local_sem.at[1]),
    ]
    for copy in own:
        copy.start()
    weights = {}
    for i, (hbm, vmem, a) in enumerate(
        ((w1_hbm, w1, 2), (w1_hbm, w1, 1), (w2_hbm, w2, 1), (w2_hbm, w2, 2), (w2_hbm, w2, 0), (w1_hbm, w1, 0))
    ):
        weights[hbm is w2_hbm, a] = pltpu.make_async_copy(hbm.at[a], vmem.at[a], local_sem.at[2 + i])
        weights[hbm is w2_hbm, a].start()

    links = {}

    def link(name, src, dst, dt, ds, via=0):
        count = len(links)
        copy = pltpu.make_async_remote_copy(
            src_ref=src, dst_ref=dst, send_sem=send_sem.at[count], recv_sem=recv_sem.at[count],
            device_id=(t + dt, s + ds), device_id_type=MESH,
        )
        links[name] = (copy, dst, inside(dt or via, ds), inside(-dt or via, -ds))

    spans = {"top": (1, 1), "bottom": (rows, 1), "upper": (2, 1), "lower": (rows - 1, 1), "second": (3, 1), "third": (4, rows - 5), "rest": (3, rows - 3)}
    for name, src, off, near_w, far_w, dt in (
        ("x", x_ref, 1, x_own, x_far, 1), ("g", g_ref, 1, g_own, g_far, -1), ("h", h_own, 0, h_own, h_far, -1)
    ):
        for part in ("top", "bottom", "upper") + (("rest",) if name == "h" else ("lower", "second", "third")):
            at, size = spans[part]
            link((name, part), src.at[:, pl.ds(at - off, size)], far_w.at[:, pl.ds(at, size)], dt, 0)
        for part, ds, to in (("top", -1, rows + 1), ("bottom", 1, 0)):
            at, size = spans[part]
            link((name, "own", to), src.at[:, pl.ds(at - off, 1)], near_w.at[:, pl.ds(to, 1)], 0, ds)
            link((name, "far", to), far_w.at[:, pl.ds(at, 1)], far_w.at[:, pl.ds(to, 1)], 0, ds, -dt)

    def send(*name):
        copy, dst, going, coming = links[name]
        pl.when(going)(copy.start)

    def arrive(*name):
        copy, dst, going, coming = links[name]
        pl.when(coming)(copy.wait_recv)

        @pl.when(jnp.logical_not(coming))
        def _():
            dst[...] = jnp.zeros(dst.shape, dst.dtype)

    def halos(name, which):
        for to in (0, rows + 1):
            arrive(name, which, to)

    def pass_on(*names):
        for part, to in (("top", rows + 1), ("bottom", 0)):
            for name in names:
                arrive(name, part)
                send(name, "far", to)

    keep_prev = (1 - clip_ref[t]).astype(F32)
    keep_next = (1 - clip_ref[jnp.minimum(t + 1, tn - 1)]).astype(F32)

    def activate(e, at, size, keep=None):
        v = xw[e:e + 2, at:at + size].astype(F32)
        v = v * sigmoid(v)
        aw[e:e + 2, at:at + size] = (v if keep is None else v * keep).astype(BF16)

    def products(buf, w, a, b, e, k, chunks):
        w, wt = w
        parts = [buf[e:e + k, at:at + n].reshape(k * n * cols, ch) for at, n in chunks]
        lhs = parts[0] if len(parts) == 1 else jnp.concatenate(parts, axis=0)
        if wt is not None and a == 2:
            dims = (((1,), (1,)), ((), ()))
            return [lax.dot_general(lhs, w[a, b, c], dims, preferred_element_type=F32) for c in range(3)]
        return [jnp.dot(lhs, (w if wt is None else wt)[a, b, c], preferred_element_type=F32) for c in range(3)]

    first, second, third = (w1, None), (w2, t2), (w1, t1)

    def turn(b, forward):
        return b if forward else 2 - b

    def store(acc, buf, w, taps, forward, fresh, at, n, keep=None):
        for a, f, e, k in taps:
            sums = None
            for b in range(3):
                new = products(buf, w, a, turn(b, forward), e, k, [(o + b, m) for o, m in zip(at, n)])
                sums = new if sums is None else [x + y for x, y in zip(sums, new)]
            put(acc, sums, f, k, list(zip(at, n)), fresh and k == 2, keep)

    def put(acc, sums, f, k, outs, fresh, keep):
        for c in range(3):
            begin = 0
            for o, n in outs:
                size = k * n * cols
                val = sums[c][begin:begin + size]
                begin += size
                if keep is not None:
                    val = val * keep
                val = val.reshape(k, n, cols, ch)
                ref = acc.at[f:f + k, o:o + n, :, c * ch:(c + 1) * ch]
                ref[...] = val if fresh else ref[...] + val

    def spread(acc, buf, w, taps, forward, sources, outs, keep=None):
        for a, f, e, k in taps:
            terms = {}
            for b in range(3):
                here = [r for r in sources if r - b in outs]
                if not here:
                    continue
                vals = products(buf, w, a, turn(b, forward), e, k, [(r, 1) for r in here])
                for at, r in enumerate(here):
                    piece = slice(at * k * cols, (at + 1) * k * cols)
                    for c in range(3):
                        terms.setdefault((c, r - b), []).append(vals[c][piece])
            for (c, o), vals in sorted(terms.items()):
                val = sum(vals[1:], vals[0])
                if keep is not None:
                    val = val * keep
                ref = acc.at[f:f + k, o, :, c * ch:(c + 1) * ch]
                ref[...] = ref[...] + val.reshape(k, cols, ch)

    def total(acc, forward, at, n):
        m = frames * n * cols
        parts = [acc[:, at:at + n, :, c * ch:(c + 1) * ch].reshape(m, ch) for c in range(3)]
        left, right = (parts[0], parts[2]) if forward else (parts[2], parts[0])
        col = lax.broadcasted_iota(jnp.int32, (m, ch), 0) % cols
        left = jnp.where(col == 0, 0.0, pltpu.roll(left, 1, 0))
        right = jnp.where(col == cols - 1, 0.0, pltpu.roll(right, m - 1, 0))
        return parts[1] + left + right

    def flip(w, wt, a):
        for b in range(3):
            for c in range(3):
                wt[a, b, c] = w[a, b, c].T

    pl.semaphore_wait(barrier, peers)
    for part in ("top", "bottom"):
        send("x", part)
        send("g", part)
    for name in ("x", "g"):
        for to in (0, rows + 1):
            send(name, "own", to)
    for copy in own:
        copy.wait()
    activate(2, 1, rows)
    halos("x", "own")
    for part in ("upper", "lower", "second", "third"):
        send("x", part)
        send("g", part)
    activate(2, 0, 1)
    activate(2, rows + 1, 1)
    weights[False, 2].wait()
    weights[False, 1].wait()
    store(acc1, aw, first, FORWARD_OWN, True, True, [0], [rows])
    weights[True, 1].wait()
    flip(w2, t2, 1)
    halos("g", "own")
    weights[True, 2].wait()
    store(acc2, gw, second, BACKWARD_OWN, False, True, [0], [rows])
    pass_on("x", "g")
    weights[True, 0].wait()
    flip(w2, t2, 0)
    weights[False, 0].wait()
    slope[...] = silu_grad(xw[2:4, 1:rows + 1].astype(F32))
    activate(0, 1, 1, keep_prev)
    activate(0, rows, 1, keep_prev)

    every = range(rows)
    edges, inside_rows = (0, last), range(1, last)
    outer = (0, 1, 2, rows - 1, rows, rows + 1)
    halos("x", "far")
    activate(0, 0, 1, keep_prev)
    activate(0, rows + 1, 1, keep_prev)
    for part, at in (("upper", 2), ("lower", rows - 1)):
        arrive("x", part)
        activate(0, at, 1, keep_prev)
    spread(acc1, aw, first, FORWARD_FAR, True, outer, edges)
    halos("g", "far")
    arrive("g", "upper")
    arrive("g", "lower")
    spread(acc2, gw, second, BACKWARD_FAR, False, outer, edges, keep_next)

    def hidden(at, n):
        hid = total(acc1, True, at, n) + bias_ref[...]
        val = total(acc2, False, at, n) * silu_grad(hid)
        hw[0:2, at + 1:at + 1 + n] = val.astype(BF16).reshape(frames, n, cols, ch)

    hidden(0, 1)
    hidden(last, 1)
    send("h", "top")
    send("h", "bottom")
    send("h", "own", rows + 1)
    send("h", "own", 0)
    most = (1, 2, 3, rows - 1, rows)
    arrive("x", "second")
    activate(0, 3, 1, keep_prev)
    spread(acc1, aw, first, FORWARD_FAR, True, most, inside_rows)
    arrive("g", "second")
    spread(acc2, gw, second, BACKWARD_FAR, False, most, inside_rows, keep_next)
    hidden(1, 1)
    send("h", "upper")
    final = range(4, rows - 1)
    arrive("x", "third")
    activate(0, 4, rows - 5, keep_prev)
    spread(acc1, aw, first, FORWARD_FAR, True, final, inside_rows)
    arrive("g", "third")
    spread(acc2, gw, second, BACKWARD_FAR, False, final, inside_rows, keep_next)
    hidden(2, rows - 3)
    send("h", "rest")

    flip(w1, t1, 1)
    halos("h", "own")
    store(acc3, hw, third, BACKWARD_OWN, False, True, [0], [rows])
    pass_on("h")
    flip(w1, t1, 0)
    arrive("h", "upper")
    halos("h", "far")
    spread(acc3, hw, third, BACKWARD_FAR, False, (0, 1, 2, rows, rows + 1), every, keep_next)

    def result(at, n):
        back = total(acc3, False, at, n).reshape(frames, n, cols, ch)
        own_g = gw[0:2, at + 1:at + 1 + n].astype(F32)
        out_ref[:, at:at + n] = (own_g + back * slope[:, at:at + n]).astype(BF16)

    result(0, 1)
    arrive("h", "rest")
    spread(acc3, hw, third, BACKWARD_FAR, False, range(3, rows), every, keep_next)
    result(1, rows - 1)
    for copy, dst, going, coming in links.values():
        pl.when(going)(copy.wait_send)


def local(features, grad_out, w_first, w_second, bias_first, clip_start):
    frames, rows, cols, ch = features.shape
    window = pltpu.VMEM((2 * frames, rows + 2, cols, ch), BF16)
    wsize = pltpu.VMEM(w_first.shape, BF16)
    acc = pltpu.VMEM((frames, rows, cols, 3 * ch), F32)
    vmem = pl.BlockSpec(memory_space=pltpu.VMEM)
    hbm = pl.BlockSpec(memory_space=pl.ANY)
    return pl.pallas_call(
        kernel,
        out_shape=pltpu.VMEM(features.shape, features.dtype),
        in_specs=[pl.BlockSpec(memory_space=pltpu.SMEM), hbm, hbm, hbm, hbm, vmem],
        out_specs=vmem,
        scratch_shapes=[
            wsize, wsize, wsize, wsize, window, window, window, window,
            acc, acc, acc, pltpu.VMEM((frames, rows, cols, ch), F32),
            pltpu.SemaphoreType.DMA((8,)),
            pltpu.SemaphoreType.DMA((28,)),
            pltpu.SemaphoreType.DMA((28,)),
        ],
        compiler_params=pltpu.CompilerParams(
            collective_id=0, has_side_effects=True, vmem_limit_bytes=54 * 1024 * 1024
        ),
    )(clip_start, features, grad_out, w_first, w_second, bias_first.reshape(1, ch))


def solution(mesh):
    placed = (P("tm", "space", None, None), P("tm", "space", None, None), P(), P(), P(), P())
    return jax.shard_map(
        local, mesh=mesh, in_specs=placed, out_specs=P("tm", "space", None, None), check_vma=False
    )
```

```python
import jax
import jax.numpy as jnp
from jax import lax
from jax.experimental import pallas as pl
from jax.experimental.pallas import tpu as pltpu
from jax.sharding import PartitionSpec as P

MESH = pl.DeviceIdType.MESH
F32 = jnp.float32
BF16 = jnp.bfloat16

FORWARD_OWN = ((2, 0, 2, 2), (1, 1, 2, 1))
FORWARD_FAR = ((0, 0, 0, 2), (1, 0, 1, 1))
BACKWARD_OWN = ((2, 0, 0, 2), (1, 0, 1, 1))
BACKWARD_FAR = ((0, 0, 2, 2), (1, 1, 2, 1))


def sigmoid(v):
    return 1.0 / (1.0 + jnp.exp(-v))


def silu_grad(v):
    s = sigmoid(v)
    return s * (1.0 + v * (1.0 - s))


def kernel(
    clip_ref, x_ref, g_ref, w1_hbm, w2_hbm, bias_ref, out_ref,
    w1, w2, t1, t2, xw, aw, gw, hw, acc1, acc2, acc3, slope, local_sem, send_sem, recv_sem,
):
    t, s = lax.axis_index("tm"), lax.axis_index("space")
    tn, sn = lax.axis_size("tm"), lax.axis_size("space")
    frames, rows, cols, ch = x_ref.shape
    last = rows - 1

    def inside(dt, ds):
        ok = None
        for d, at, size in ((dt, t, tn), (ds, s, sn)):
            if d:
                term = (at + d >= 0) if d < 0 else (at + d < size)
                ok = term if ok is None else jnp.logical_and(ok, term)
        return ok

    barrier = pltpu.get_barrier_semaphore()
    peers = 0
    for dt, ds in ((1, 0), (-1, 0), (0, 1), (0, -1)):
        @pl.when(inside(dt, ds))
        def _(dt=dt, ds=ds):
            pl.semaphore_signal(barrier, inc=1, device_id=(t + dt, s + ds), device_id_type=MESH)
        peers = peers + inside(dt, ds).astype(jnp.int32)

    x_own, g_own, h_own = xw.at[2:4], gw.at[0:2], hw.at[0:2]
    x_far, g_far, h_far = xw.at[0:2], gw.at[2:4], hw.at[2:4]
    inner = pl.ds(1, rows)
    own = [
        pltpu.make_async_copy(x_ref, x_own.at[:, inner], local_sem.at[0]),
        pltpu.make_async_copy(g_ref, g_own.at[:, inner], local_sem.at[1]),
    ]
    for copy in own:
        copy.start()
    weights = {}
    for i, (hbm, vmem, a) in enumerate(
        ((w1_hbm, w1, 2), (w1_hbm, w1, 1), (w2_hbm, w2, 1), (w2_hbm, w2, 2), (w2_hbm, w2, 0), (w1_hbm, w1, 0))
    ):
        weights[hbm is w2_hbm, a] = pltpu.make_async_copy(hbm.at[a], vmem.at[a], local_sem.at[2 + i])
        weights[hbm is w2_hbm, a].start()

    links = {}

    def link(name, src, dst, dt, ds, via=0):
        count = len(links)
        copy = pltpu.make_async_remote_copy(
            src_ref=src, dst_ref=dst, send_sem=send_sem.at[count], recv_sem=recv_sem.at[count],
            device_id=(t + dt, s + ds), device_id_type=MESH,
        )
        links[name] = (copy, dst, inside(dt or via, ds), inside(-dt or via, -ds))

    spans = {"top": (1, 1), "bottom": (rows, 1), "upper": (2, 1), "lower": (rows - 1, 1), "second": (3, 1), "third": (4, rows - 5), "middle": (3, rows - 4)}
    for name, src, off, near_w, far_w, dt in (
        ("x", x_ref, 1, x_own, x_far, 1), ("g", g_ref, 1, g_own, g_far, -1), ("h", h_own, 0, h_own, h_far, -1)
    ):
        for part in ("top", "bottom", "upper") + (("lower", "middle") if name == "h" else ("lower", "second", "third")):
            at, size = spans[part]
            link((name, part), src.at[:, pl.ds(at - off, size)], far_w.at[:, pl.ds(at, size)], dt, 0)
        for part, ds, to in (("top", -1, rows + 1), ("bottom", 1, 0)):
            at, size = spans[part]
            link((name, "own", to), src.at[:, pl.ds(at - off, 1)], near_w.at[:, pl.ds(to, 1)], 0, ds)
            link((name, "far", to), far_w.at[:, pl.ds(at, 1)], far_w.at[:, pl.ds(to, 1)], 0, ds, -dt)

    def send(*name):
        copy, dst, going, coming = links[name]
        pl.when(going)(copy.start)

    def arrive(*name):
        copy, dst, going, coming = links[name]
        pl.when(coming)(copy.wait_recv)

        @pl.when(jnp.logical_not(coming))
        def _():
            dst[...] = jnp.zeros(dst.shape, dst.dtype)

    def halos(name, which):
        for to in (0, rows + 1):
            arrive(name, which, to)

    def pass_on(*names):
        for part, to in (("top", rows + 1), ("bottom", 0)):
            for name in names:
                arrive(name, part)
                send(name, "far", to)

    keep_prev = (1 - clip_ref[t]).astype(F32)
    keep_next = (1 - clip_ref[jnp.minimum(t + 1, tn - 1)]).astype(F32)

    def activate(e, at, size, keep=None):
        v = xw[e:e + 2, at:at + size].astype(F32)
        v = v * sigmoid(v)
        aw[e:e + 2, at:at + size] = (v if keep is None else v * keep).astype(BF16)

    def products(buf, w, a, b, e, k, chunks):
        w, wt = w
        parts = [buf[e:e + k, at:at + n].reshape(k * n * cols, ch) for at, n in chunks]
        lhs = parts[0] if len(parts) == 1 else jnp.concatenate(parts, axis=0)
        if wt is not None and a == 2:
            dims = (((1,), (1,)), ((), ()))
            return [lax.dot_general(lhs, w[a, b, c], dims, preferred_element_type=F32) for c in range(3)]
        return [jnp.dot(lhs, (w if wt is None else wt)[a, b, c], preferred_element_type=F32) for c in range(3)]

    first, second, third = (w1, None), (w2, t2), (w1, t1)

    def turn(b, forward):
        return b if forward else 2 - b

    def store(acc, buf, w, taps, forward, fresh, at, n, keep=None):
        for a, f, e, k in taps:
            sums = None
            for b in range(3):
                new = products(buf, w, a, turn(b, forward), e, k, [(o + b, m) for o, m in zip(at, n)])
                sums = new if sums is None else [x + y for x, y in zip(sums, new)]
            put(acc, sums, f, k, list(zip(at, n)), fresh and k == 2, keep)

    def put(acc, sums, f, k, outs, fresh, keep):
        for c in range(3):
            begin = 0
            for o, n in outs:
                size = k * n * cols
                val = sums[c][begin:begin + size]
                begin += size
                if keep is not None:
                    val = val * keep
                val = val.reshape(k, n, cols, ch)
                ref = acc.at[f:f + k, o:o + n, :, c * ch:(c + 1) * ch]
                ref[...] = val if fresh else ref[...] + val

    def spread(acc, buf, w, taps, forward, sources, outs, keep=None):
        for a, f, e, k in taps:
            terms = {}
            for b in range(3):
                here = [r for r in sources if r - b in outs]
                if not here:
                    continue
                vals = products(buf, w, a, turn(b, forward), e, k, [(r, 1) for r in here])
                for at, r in enumerate(here):
                    piece = slice(at * k * cols, (at + 1) * k * cols)
                    for c in range(3):
                        terms.setdefault((c, r - b), []).append(vals[c][piece])
            for (c, o), vals in sorted(terms.items()):
                val = sum(vals[1:], vals[0])
                if keep is not None:
                    val = val * keep
                ref = acc.at[f:f + k, o, :, c * ch:(c + 1) * ch]
                ref[...] = ref[...] + val.reshape(k, cols, ch)

    def total(acc, forward, at, n):
        m = frames * n * cols
        parts = [acc[:, at:at + n, :, c * ch:(c + 1) * ch].reshape(m, ch) for c in range(3)]
        left, right = (parts[0], parts[2]) if forward else (parts[2], parts[0])
        col = lax.broadcasted_iota(jnp.int32, (m, ch), 0) % cols
        left = jnp.where(col == 0, 0.0, pltpu.roll(left, 1, 0))
        right = jnp.where(col == cols - 1, 0.0, pltpu.roll(right, m - 1, 0))
        return parts[1] + left + right

    def flip(w, wt, a):
        for b in range(3):
            for c in range(3):
                wt[a, b, c] = w[a, b, c].T

    pl.semaphore_wait(barrier, peers)
    for part in ("top", "bottom"):
        send("x", part)
        send("g", part)
    for name in ("x", "g"):
        for to in (0, rows + 1):
            send(name, "own", to)
    for copy in own:
        copy.wait()
    activate(2, 1, rows)
    slope[...] = silu_grad(xw[2:4, 1:rows + 1].astype(F32))
    halos("x", "own")
    for part in ("upper", "lower", "second", "third"):
        send("x", part)
        send("g", part)
    activate(2, 0, 1)
    activate(2, rows + 1, 1)
    weights[False, 2].wait()
    weights[False, 1].wait()
    store(acc1, aw, first, FORWARD_OWN, True, True, [0], [rows])
    weights[True, 1].wait()
    flip(w2, t2, 1)
    halos("g", "own")
    weights[True, 2].wait()
    store(acc2, gw, second, BACKWARD_OWN, False, True, [0], [rows])
    pass_on("x", "g")
    flip(w1, t1, 1)
    weights[True, 0].wait()
    flip(w2, t2, 0)
    weights[False, 0].wait()
    activate(0, 1, 1, keep_prev)
    activate(0, rows, 1, keep_prev)

    every = range(rows)
    edges, inside_rows = (0, last), range(1, last)
    outer = (0, 1, 2, rows - 1, rows, rows + 1)
    halos("x", "far")
    activate(0, 0, 1, keep_prev)
    activate(0, rows + 1, 1, keep_prev)
    for part, at in (("upper", 2), ("lower", rows - 1)):
        arrive("x", part)
        activate(0, at, 1, keep_prev)
    spread(acc1, aw, first, FORWARD_FAR, True, outer, edges)
    halos("g", "far")
    arrive("g", "upper")
    arrive("g", "lower")
    spread(acc2, gw, second, BACKWARD_FAR, False, outer, edges, keep_next)

    def hidden(at, n):
        hid = total(acc1, True, at, n) + bias_ref[...]
        val = total(acc2, False, at, n) * silu_grad(hid)
        hw[0:2, at + 1:at + 1 + n] = val.astype(BF16).reshape(frames, n, cols, ch)

    hidden(0, 1)
    hidden(last, 1)
    send("h", "top")
    send("h", "bottom")
    send("h", "own", rows + 1)
    send("h", "own", 0)
    most = (1, 2, 3, rows - 1, rows)
    arrive("x", "second")
    activate(0, 3, 1, keep_prev)
    spread(acc1, aw, first, FORWARD_FAR, True, most, inside_rows)
    arrive("g", "second")
    spread(acc2, gw, second, BACKWARD_FAR, False, most, inside_rows, keep_next)
    hidden(1, 1)
    send("h", "upper")
    final = range(4, rows - 1)
    arrive("x", "third")
    activate(0, 4, rows - 5, keep_prev)
    spread(acc1, aw, first, FORWARD_FAR, True, final, inside_rows)
    arrive("g", "third")
    spread(acc2, gw, second, BACKWARD_FAR, False, final, inside_rows, keep_next)
    hidden(2, rows - 3)
    send("h", "lower")
    send("h", "middle")

    halos("h", "own")
    store(acc3, hw, third, BACKWARD_OWN, False, True, [0], [rows])
    pass_on("h")
    flip(w1, t1, 0)
    arrive("h", "upper")
    halos("h", "far")
    arrive("h", "lower")
    spread(acc3, hw, third, BACKWARD_FAR, False, outer, every, keep_next)

    def result(at, n):
        back = total(acc3, False, at, n).reshape(frames, n, cols, ch)
        own_g = gw[0:2, at + 1:at + 1 + n].astype(F32)
        out_ref[:, at:at + n] = (own_g + back * slope[:, at:at + n]).astype(BF16)

    result(0, 1)
    result(last, 1)
    arrive("h", "middle")
    spread(acc3, hw, third, BACKWARD_FAR, False, range(3, rows - 1), every, keep_next)
    result(1, rows - 2)
    for copy, dst, going, coming in links.values():
        pl.when(going)(copy.wait_send)


def local(features, grad_out, w_first, w_second, bias_first, clip_start):
    frames, rows, cols, ch = features.shape
    window = pltpu.VMEM((2 * frames, rows + 2, cols, ch), BF16)
    wsize = pltpu.VMEM(w_first.shape, BF16)
    acc = pltpu.VMEM((frames, rows, cols, 3 * ch), F32)
    vmem = pl.BlockSpec(memory_space=pltpu.VMEM)
    hbm = pl.BlockSpec(memory_space=pl.ANY)
    return pl.pallas_call(
        kernel,
        out_shape=pltpu.VMEM(features.shape, features.dtype),
        in_specs=[pl.BlockSpec(memory_space=pltpu.SMEM), hbm, hbm, hbm, hbm, vmem],
        out_specs=vmem,
        scratch_shapes=[
            wsize, wsize, wsize, wsize, window, window, window, window,
            acc, acc, acc, pltpu.VMEM((frames, rows, cols, ch), F32),
            pltpu.SemaphoreType.DMA((8,)),
            pltpu.SemaphoreType.DMA((29,)),
            pltpu.SemaphoreType.DMA((29,)),
        ],
        compiler_params=pltpu.CompilerParams(
            collective_id=0, has_side_effects=True, vmem_limit_bytes=54 * 1024 * 1024
        ),
    )(clip_start, features, grad_out, w_first, w_second, bias_first.reshape(1, ch))


def solution(mesh):
    placed = (P("tm", "space", None, None), P("tm", "space", None, None), P(), P(), P(), P())
    return jax.shard_map(
        local, mesh=mesh, in_specs=placed, out_specs=P("tm", "space", None, None), check_vma=False
    )
```

```python
import jax
import jax.numpy as jnp
from jax import lax
from jax.experimental import pallas as pl
from jax.experimental.pallas import tpu as pltpu
from jax.sharding import PartitionSpec as P

MESH = pl.DeviceIdType.MESH
F32 = jnp.float32
BF16 = jnp.bfloat16

FORWARD_OWN = ((2, 0, 2, 2), (1, 1, 2, 1))
FORWARD_FAR = ((0, 0, 0, 2), (1, 0, 1, 1))
BACKWARD_OWN = ((2, 0, 0, 2), (1, 0, 1, 1))
BACKWARD_FAR = ((0, 0, 2, 2), (1, 1, 2, 1))


def sigmoid(v):
    return 1.0 / (1.0 + jnp.exp(-v))


def silu_grad(v):
    s = sigmoid(v)
    return s * (1.0 + v * (1.0 - s))


def kernel(
    clip_ref, x_ref, g_ref, w1_hbm, w2_hbm, bias_ref, out_ref,
    w1, w2, t1, t2, xw, aw, gw, hw, acc1, acc2, acc3, slope, local_sem, send_sem, recv_sem,
):
    t, s = lax.axis_index("tm"), lax.axis_index("space")
    tn, sn = lax.axis_size("tm"), lax.axis_size("space")
    frames, rows, cols, ch = x_ref.shape
    last = rows - 1

    def inside(dt, ds):
        ok = None
        for d, at, size in ((dt, t, tn), (ds, s, sn)):
            if d:
                term = (at + d >= 0) if d < 0 else (at + d < size)
                ok = term if ok is None else jnp.logical_and(ok, term)
        return ok

    barrier = pltpu.get_barrier_semaphore()
    peers = 0
    for dt, ds in ((1, 0), (-1, 0), (0, 1), (0, -1)):
        @pl.when(inside(dt, ds))
        def _(dt=dt, ds=ds):
            pl.semaphore_signal(barrier, inc=1, device_id=(t + dt, s + ds), device_id_type=MESH)
        peers = peers + inside(dt, ds).astype(jnp.int32)

    x_own, g_own, h_own = xw.at[2:4], gw.at[0:2], hw.at[0:2]
    x_far, g_far, h_far = xw.at[0:2], gw.at[2:4], hw.at[2:4]
    inner = pl.ds(1, rows)
    own = [
        pltpu.make_async_copy(x_ref, x_own.at[:, inner], local_sem.at[0]),
        pltpu.make_async_copy(g_ref, g_own.at[:, inner], local_sem.at[1]),
    ]
    for copy in own:
        copy.start()
    weights = {}
    for i, (hbm, vmem, a) in enumerate(
        ((w1_hbm, w1, 2), (w1_hbm, w1, 1), (w2_hbm, w2, 1), (w2_hbm, w2, 2), (w2_hbm, w2, 0), (w1_hbm, w1, 0))
    ):
        weights[hbm is w2_hbm, a] = pltpu.make_async_copy(hbm.at[a], vmem.at[a], local_sem.at[2 + i])
        weights[hbm is w2_hbm, a].start()

    links = {}

    def link(name, src, dst, dt, ds, via=0):
        count = len(links)
        copy = pltpu.make_async_remote_copy(
            src_ref=src, dst_ref=dst, send_sem=send_sem.at[count], recv_sem=recv_sem.at[count],
            device_id=(t + dt, s + ds), device_id_type=MESH,
        )
        links[name] = (copy, dst, inside(dt or via, ds), inside(-dt or via, -ds))

    spans = {"top": (1, 1), "bottom": (rows, 1), "upper": (2, 1), "lower": (rows - 1, 1), "second": (3, 1), "third": (4, rows - 5), "middle": (3, rows - 4)}
    for name, src, off, near_w, far_w, dt in (
        ("x", x_ref, 1, x_own, x_far, 1), ("g", g_ref, 1, g_own, g_far, -1), ("h", h_own, 0, h_own, h_far, -1)
    ):
        for part in ("top", "bottom", "upper") + (("lower", "middle") if name == "h" else ("lower", "second", "third")):
            at, size = spans[part]
            link((name, part), src.at[:, pl.ds(at - off, size)], far_w.at[:, pl.ds(at, size)], dt, 0)
        for part, ds, to in (("top", -1, rows + 1), ("bottom", 1, 0)):
            at, size = spans[part]
            link((name, "own", to), src.at[:, pl.ds(at - off, 1)], near_w.at[:, pl.ds(to, 1)], 0, ds)
            link((name, "far", to), far_w.at[:, pl.ds(at, 1)], far_w.at[:, pl.ds(to, 1)], 0, ds, -dt)

    def send(*name):
        copy, dst, going, coming = links[name]
        pl.when(going)(copy.start)

    def arrive(*name):
        copy, dst, going, coming = links[name]
        pl.when(coming)(copy.wait_recv)

        @pl.when(jnp.logical_not(coming))
        def _():
            dst[...] = jnp.zeros(dst.shape, dst.dtype)

    def halos(name, which):
        for to in (0, rows + 1):
            arrive(name, which, to)

    def pass_on(*names):
        for part, to in (("top", rows + 1), ("bottom", 0)):
            for name in names:
                arrive(name, part)
                send(name, "far", to)

    keep_prev = (1 - clip_ref[t]).astype(F32)
    keep_next = (1 - clip_ref[jnp.minimum(t + 1, tn - 1)]).astype(F32)

    def activate(e, at, size, keep=None):
        v = xw[e:e + 2, at:at + size].astype(F32)
        v = v * sigmoid(v)
        aw[e:e + 2, at:at + size] = (v if keep is None else v * keep).astype(BF16)

    def products(buf, w, a, b, e, k, chunks):
        w, wt = w
        parts = [buf[e:e + k, at:at + n].reshape(k * n * cols, ch) for at, n in chunks]
        lhs = parts[0] if len(parts) == 1 else jnp.concatenate(parts, axis=0)
        if wt is not None and a == 2:
            dims = (((1,), (1,)), ((), ()))
            return [lax.dot_general(lhs, w[a, b, c], dims, preferred_element_type=F32) for c in range(3)]
        return [jnp.dot(lhs, (w if wt is None else wt)[a, b, c], preferred_element_type=F32) for c in range(3)]

    first, second, third = (w1, None), (w2, t2), (w1, t1)

    def turn(b, forward):
        return b if forward else 2 - b

    def store(acc, buf, w, taps, forward, fresh, at, n, keep=None):
        for a, f, e, k in taps:
            sums = None
            for b in range(3):
                new = products(buf, w, a, turn(b, forward), e, k, [(o + b, m) for o, m in zip(at, n)])
                sums = new if sums is None else [x + y for x, y in zip(sums, new)]
            put(acc, sums, f, k, list(zip(at, n)), fresh and k == 2, keep)

    def put(acc, sums, f, k, outs, fresh, keep):
        for c in range(3):
            begin = 0
            for o, n in outs:
                size = k * n * cols
                val = sums[c][begin:begin + size]
                begin += size
                if keep is not None:
                    val = val * keep
                val = val.reshape(k, n, cols, ch)
                ref = acc.at[f:f + k, o:o + n, :, c * ch:(c + 1) * ch]
                ref[...] = val if fresh else ref[...] + val

    def spread(acc, buf, w, taps, forward, sources, outs, keep=None):
        for a, f, e, k in taps:
            terms = {}
            for b in range(3):
                here = [r for r in sources if r - b in outs]
                if not here:
                    continue
                vals = products(buf, w, a, turn(b, forward), e, k, [(r, 1) for r in here])
                for at, r in enumerate(here):
                    piece = slice(at * k * cols, (at + 1) * k * cols)
                    for c in range(3):
                        terms.setdefault((c, r - b), []).append(vals[c][piece])
            for (c, o), vals in sorted(terms.items()):
                val = sum(vals[1:], vals[0])
                if keep is not None:
                    val = val * keep
                ref = acc.at[f:f + k, o, :, c * ch:(c + 1) * ch]
                ref[...] = ref[...] + val.reshape(k, cols, ch)

    def total(acc, forward, at, n):
        m = frames * n * cols
        parts = [acc[:, at:at + n, :, c * ch:(c + 1) * ch].reshape(m, ch) for c in range(3)]
        left, right = (parts[0], parts[2]) if forward else (parts[2], parts[0])
        col = lax.broadcasted_iota(jnp.int32, (m, ch), 0) % cols
        left = jnp.where(col == 0, 0.0, pltpu.roll(left, 1, 0))
        right = jnp.where(col == cols - 1, 0.0, pltpu.roll(right, m - 1, 0))
        return parts[1] + left + right

    def flip(w, wt, a):
        for b in range(3):
            for c in range(3):
                wt[a, b, c] = w[a, b, c].T

    pl.semaphore_wait(barrier, peers)
    for part in ("top", "bottom"):
        send("x", part)
        send("g", part)
    for name in ("x", "g"):
        for to in (0, rows + 1):
            send(name, "own", to)
    for copy in own:
        copy.wait()
    activate(2, 1, rows)
    slope[...] = silu_grad(xw[2:4, 1:rows + 1].astype(F32))
    halos("x", "own")
    for part in ("upper", "lower", "second", "third"):
        send("x", part)
        send("g", part)
    activate(2, 0, 1)
    activate(2, rows + 1, 1)
    weights[False, 2].wait()
    weights[False, 1].wait()
    store(acc1, aw, first, FORWARD_OWN, True, True, [0], [rows])
    weights[True, 1].wait()
    flip(w2, t2, 1)
    halos("g", "own")
    weights[True, 2].wait()
    store(acc2, gw, second, BACKWARD_OWN, False, True, [0], [rows])
    pass_on("x", "g")
    flip(w1, t1, 1)
    weights[True, 0].wait()
    flip(w2, t2, 0)
    weights[False, 0].wait()
    activate(0, 1, 1, keep_prev)
    activate(0, rows, 1, keep_prev)

    every = range(rows)
    edges, inside_rows = (0, last), range(1, last)
    outer = (0, 1, 2, rows - 1, rows, rows + 1)
    halos("x", "far")
    activate(0, 0, 1, keep_prev)
    activate(0, rows + 1, 1, keep_prev)
    for part, at in (("upper", 2), ("lower", rows - 1)):
        arrive("x", part)
        activate(0, at, 1, keep_prev)
    spread(acc1, aw, first, FORWARD_FAR, True, outer, edges)
    halos("g", "far")
    arrive("g", "upper")
    arrive("g", "lower")
    spread(acc2, gw, second, BACKWARD_FAR, False, outer, edges, keep_next)

    def hidden(at, n):
        hid = total(acc1, True, at, n) + bias_ref[...]
        val = total(acc2, False, at, n) * silu_grad(hid)
        hw[0:2, at + 1:at + 1 + n] = val.astype(BF16).reshape(frames, n, cols, ch)

    hidden(0, 1)
    send("h", "top")
    send("h", "own", rows + 1)
    hidden(last, 1)
    send("h", "bottom")
    send("h", "own", 0)
    most = (1, 2, 3, rows - 1, rows)
    arrive("x", "second")
    activate(0, 3, 1, keep_prev)
    spread(acc1, aw, first, FORWARD_FAR, True, most, inside_rows)
    arrive("g", "second")
    spread(acc2, gw, second, BACKWARD_FAR, False, most, inside_rows, keep_next)
    hidden(1, 1)
    send("h", "upper")
    final = range(4, rows - 1)
    arrive("x", "third")
    activate(0, 4, rows - 5, keep_prev)
    spread(acc1, aw, first, FORWARD_FAR, True, final, inside_rows)
    arrive("g", "third")
    spread(acc2, gw, second, BACKWARD_FAR, False, final, inside_rows, keep_next)
    hidden(last - 1, 1)
    send("h", "lower")
    hidden(2, rows - 4)
    send("h", "middle")

    halos("h", "own")
    store(acc3, hw, third, BACKWARD_OWN, False, True, [0], [rows])
    pass_on("h")
    flip(w1, t1, 0)
    arrive("h", "upper")
    halos("h", "far")
    arrive("h", "lower")
    spread(acc3, hw, third, BACKWARD_FAR, False, outer, every, keep_next)

    def result(at, n):
        back = total(acc3, False, at, n).reshape(frames, n, cols, ch)
        own_g = gw[0:2, at + 1:at + 1 + n].astype(F32)
        out_ref[:, at:at + n] = (own_g + back * slope[:, at:at + n]).astype(BF16)

    result(0, 1)
    result(last, 1)
    arrive("h", "middle")
    spread(acc3, hw, third, BACKWARD_FAR, False, range(3, rows - 1), every, keep_next)
    result(1, rows - 2)
    for copy, dst, going, coming in links.values():
        pl.when(going)(copy.wait_send)


def local(features, grad_out, w_first, w_second, bias_first, clip_start):
    frames, rows, cols, ch = features.shape
    window = pltpu.VMEM((2 * frames, rows + 2, cols, ch), BF16)
    wsize = pltpu.VMEM(w_first.shape, BF16)
    acc = pltpu.VMEM((frames, rows, cols, 3 * ch), F32)
    vmem = pl.BlockSpec(memory_space=pltpu.VMEM)
    hbm = pl.BlockSpec(memory_space=pl.ANY)
    return pl.pallas_call(
        kernel,
        out_shape=pltpu.VMEM(features.shape, features.dtype),
        in_specs=[pl.BlockSpec(memory_space=pltpu.SMEM), hbm, hbm, hbm, hbm, vmem],
        out_specs=vmem,
        scratch_shapes=[
            wsize, wsize, wsize, wsize, window, window, window, window,
            acc, acc, acc, pltpu.VMEM((frames, rows, cols, ch), F32),
            pltpu.SemaphoreType.DMA((8,)),
            pltpu.SemaphoreType.DMA((29,)),
            pltpu.SemaphoreType.DMA((29,)),
        ],
        compiler_params=pltpu.CompilerParams(
            collective_id=0, has_side_effects=True, vmem_limit_bytes=54 * 1024 * 1024
        ),
    )(clip_start, features, grad_out, w_first, w_second, bias_first.reshape(1, ch))


def solution(mesh):
    placed = (P("tm", "space", None, None), P("tm", "space", None, None), P(), P(), P(), P())
    return jax.shard_map(
        local, mesh=mesh, in_specs=placed, out_specs=P("tm", "space", None, None), check_vma=False
    )
```
